256 devices in a mesh: req: 32 (over x, y, core), tp: 8 (over z).
Axes of the slice: x: 4, y: 4, z: 8, core: 2. Of those that a mesh axis runs over, the one named last changes fastest.
Arguments:
- hidden: bfloat16 [8192, 5120], P('req', 'tp'), may hold values from -8 to 8
- q_new: bfloat16 [8192, 5120], P('req', 'tp'), may hold values from -8 to 8
- k_new: bfloat16 [8192, 5120], P('req', 'tp'), may hold values from -8 to 8
- v_new: bfloat16 [8192, 5120], P('req', 'tp'), may hold values from -8 to 8
- cache_k: bfloat16 [32, 4096, 5120], P('req', None, 'tp'), may hold values from -8 to 8
- cache_v: bfloat16 [32, 4096, 5120], P('req', None, 'tp'), may hold values from -8 to 8
- cache_len: int32 [32], replicated, may hold values from 1 to 4096, 32768 in all
- w_out: bfloat16 [5120, 5120], P('tp', 'req'), may hold values from -0.625 to 0.625
- q_cross: bfloat16 [8192, 5120], P('req', 'tp'), may hold values from -8 to 8
- text_k: bfloat16 [4, 512, 5120], P(None, 'req', 'tp'), may hold values from -8 to 8
- text_v: bfloat16 [4, 512, 5120], P(None, 'req', 'tp'), may hold values from -12 to 12
- prompt_of: int32 [32], P('req'), may hold values from 0 to 3, as said below
Outputs:
- hidden_out: bfloat16 [8192, 5120], P('req', 'tp')
- cross_heads: bfloat16 [8192, 5120], P('req', 'tp')
The draws below stay inside these ranges and needn't reach their ends.
Inputs may be any that keep to these rules, and one draw needn't show every extreme that they name: `cache_len`: cache rows at or beyond a request's length hold no data; the longest request fills all 4096 rows. `prompt_of`: each of the 4 prompts serves exactly 8 requests.
All inputs are finite; a program needn't handle non-finite values.
Results may differ from the reference program's by a relative error of at most 0.014.
Values may be sent and summed in bfloat16 or wider, within the bound.
A program may use at most 128 MiB of HBM per device.

```python
import math
import jax
import jax.numpy as jnp
import numpy as np
from jax import lax

D = 5120
HEADS = 40
HD = 128
TEXT = 512
NEW = 256
CACHE = 4096
PROMPTS = 4
F = 5120
REQS = 32
TOKENS = 8192


def shared_signs(key):
    base_key = jax.random.fold_in(key, 101)
    key_order = jax.random.fold_in(base_key, 0)
    prompt_ids = (jax.random.permutation(key_order, REQS) % PROMPTS).astype(jnp.int32)
    return prompt_ids


def rough_normal(key, tag, shape):
    return jnp.clip(jax.random.normal(jax.random.fold_in(key, tag), shape, jnp.float32), -8.0, 8.0)


def draw_q_new(key, part):
    values = rough_normal(key, 1, (REQS, NEW, F))
    return values.reshape(TOKENS, F).astype(jnp.bfloat16)


def draw_k_new(key, part):
    values = rough_normal(key, 2, (REQS, NEW, F))
    return values.reshape(TOKENS, F).astype(jnp.bfloat16)


def draw_cache_k(key, part):
    values = rough_normal(key, 3, (REQS, CACHE, F))
    return values.astype(jnp.bfloat16)


def draw_q_cross(key, part):
    values = rough_normal(key, 4, (REQS, NEW, F))
    return values.reshape(TOKENS, F).astype(jnp.bfloat16)


def draw_text_k(key, part):
    values = rough_normal(key, 5, (PROMPTS, TEXT, F))
    return values.astype(jnp.bfloat16)


def draw_prompt_of(key, part):
    return shared_signs(key)


def steps_of(own_key, extent, shards, least, largest):
    gain = 1.0
    for axis_at, parts in shards:
        heights = jax.random.uniform(jax.random.fold_in(jax.random.fold_in(own_key, 6), axis_at), (parts,), jnp.float32, least / len(shards), largest / len(shards))
        gain = gain * jnp.repeat(jnp.exp(heights), extent[axis_at] // parts).reshape((-1,) + (1,) * (len(extent) - 1 - axis_at))
    return gain


def length_profile(count, total, reach, slope):
    loads = [(1 << 20) // math.isqrt(grade ** slope) + 1 for grade in range(2, count + 1)]
    spare, given = total - reach - (count - 1), [1] * (count - 1)
    while spare > 0:
        free = [i for i in range(count - 1) if given[i] < reach]
        whole, budget = sum([loads[i] for i in free]), spare
        for i in free:
            extra = min(reach - given[i], max(1, budget * loads[i] // whole), spare)
            given[i] = given[i] + extra
            spare = spare - extra
    return np.array([reach] + given)


def uneven_parts(own_key, amount, total, reach, lean):
    if amount == 2:
        one = jax.random.randint(own_key, (), max(1, total - reach), min(reach, total - 1) + 1)
        return jnp.stack([one, total - one])
    tallies = jnp.asarray(length_profile(amount, total, reach, lean), jnp.int32)
    pairs = (amount - 1) // 2
    source_of, receiver = tallies[1:1 + 2 * pairs:2], tallies[2:2 + 2 * pairs:2]
    room = jnp.minimum(source_of - 1, reach - receiver)
    moved = jax.random.randint(jax.random.fold_in(own_key, 1), (pairs,), 0, 1 << 20) % (room + 1)
    tallies = tallies.at[1:1 + 2 * pairs:2].set(source_of - moved).at[2:2 + 2 * pairs:2].set(receiver + moved)
    return tallies[jax.random.permutation(jax.random.fold_in(own_key, 2), amount)]


def scatter_about(own_key, dims, width, most, pieces=(), kind=jnp.bfloat16):
    result = jax.random.normal(own_key, dims, jnp.float32) * width
    if len(pieces) > 0:
        result = steps_of(own_key, dims, pieces, -0.22, 0.18) * result
    return jnp.clip(result, min=-most, max=most).astype(kind)


def setup_inputs(seed: int = 0) -> dict:
    key_list = jax.random.split(jax.random.key(seed), 13)
    hidden = scatter_about(key_list[0], (TOKENS, D), 1.0, 8.0, ((0, 32), (1, 8)))
    q_new = draw_q_new(jax.random.fold_in(key_list[12], 71), 0)
    k_new = draw_k_new(jax.random.fold_in(key_list[12], 71), 0)
    v_new = scatter_about(key_list[3], (TOKENS, F), 1.0, 8.0, ((0, 32), (1, 8)))
    cache_k = draw_cache_k(jax.random.fold_in(key_list[12], 71), 0)
    cache_v = scatter_about(key_list[5], (REQS, CACHE, F), 1.0, 8.0, ((0, 32), (2, 8)))
    cache_len = uneven_parts(key_list[6], REQS, REQS * CACHE // 4, CACHE, 2).astype(jnp.int32)
    w_out = scatter_about(key_list[7], (F, D), (F // 64) ** -0.5, 0.625, ((0, 8), (1, 32)))
    q_cross = draw_q_cross(jax.random.fold_in(key_list[12], 71), 0)
    text_k = draw_text_k(jax.random.fold_in(key_list[12], 71), 0)
    text_v = scatter_about(key_list[10], (PROMPTS, TEXT, F), 2.0, 12.0, ((1, 32), (2, 8)))
    prompt_of = draw_prompt_of(jax.random.fold_in(key_list[12], 71), 0)
    return dict(hidden=hidden, q_new=q_new, k_new=k_new, v_new=v_new, cache_k=cache_k, cache_v=cache_v, cache_len=cache_len, w_out=w_out, q_cross=q_cross, text_k=text_k, text_v=text_v, prompt_of=prompt_of)


NEG_FILL = -1e30


def attend_all(queries, keys, values, visible):
    scores = jnp.einsum("qhd,khd->hqk", queries.astype(jnp.float32), keys.astype(jnp.float32)) * (HD ** -0.5)
    scores = jnp.where(visible[None], scores, NEG_FILL)
    maxima = jnp.max(scores, axis=-1, keepdims=True)
    weights = jnp.where(visible[None], jnp.exp(scores - maxima), jnp.float32(0.0))
    masses = jnp.sum(weights, axis=-1)
    rounded = lax.optimization_barrier(weights.astype(jnp.bfloat16))
    output = jnp.einsum("hqk,khd->hqd", rounded.astype(jnp.float32), values.astype(jnp.float32)) / masses[..., None]
    return output.transpose(1, 0, 2).reshape(queries.shape[0], HEADS * HD).astype(jnp.bfloat16)


def reference(hidden, q_new, k_new, v_new, cache_k, cache_v, cache_len, w_out, q_cross, text_k, text_v, prompt_of):
    def self_request(items):
        queries, new_keys, new_values, old_keys, old_values, length = items
        keys = jnp.concatenate([old_keys, new_keys], axis=0).reshape(CACHE + NEW, HEADS, HD)
        values = jnp.concatenate([old_values, new_values], axis=0).reshape(CACHE + NEW, HEADS, HD)
        row_ids = jnp.arange(NEW, dtype=jnp.int32)[:, None]
        col_ids = jnp.arange(CACHE + NEW, dtype=jnp.int32)[None, :]
        visible = jnp.where(col_ids < CACHE, col_ids < length, (col_ids - CACHE) <= row_ids)
        return attend_all(queries.reshape(NEW, HEADS, HD), keys, values, visible)

    self_heads = lax.map(self_request, (q_new.reshape(REQS, NEW, F), k_new.reshape(REQS, NEW, F), v_new.reshape(REQS, NEW, F), cache_k, cache_v, cache_len))
    self_heads = self_heads.reshape(TOKENS, F)
    projected = jnp.dot(self_heads, w_out, preferred_element_type=jnp.float32)
    hidden_out = (hidden.astype(jnp.float32) + projected).astype(jnp.bfloat16)

    def cross_request(items):
        queries, prompt = items
        keys = jnp.take(text_k, prompt, axis=0).reshape(TEXT, HEADS, HD)
        values = jnp.take(text_v, prompt, axis=0).reshape(TEXT, HEADS, HD)
        visible = jnp.ones((NEW, TEXT), dtype=bool)
        return attend_all(queries.reshape(NEW, HEADS, HD), keys, values, visible)

    cross_heads = lax.map(cross_request, (q_cross.reshape(REQS, NEW, F), prompt_of)).reshape(TOKENS, F)
    return hidden_out, cross_heads
```

```python
import jax
import jax.numpy as jnp
from jax import lax
from jax.experimental import pallas as pl
from jax.experimental.pallas import tpu as pltpu
from jax.sharding import PartitionSpec as P

MESH = pl.DeviceIdType.MESH
HD = 128
NH = 5
ROWS = 256
W = NH * HD
CAP = 4096
KEYS = CAP + ROWS
CHUNK = 512
NEG = -1e30
SCALE = HD**-0.5
LOG2E = 1.4426950408889634
NT = (((1,), (1,)), ((), ()))
F32 = jnp.float32
BF16 = jnp.bfloat16


def kernel(
    len_ref, prompt_ref, hid_h, q_h, kn_h, vn_h, ck_h, cv_h, w_h, qc_h, tk_h, tv_h,
    out_h, cross_h,
    q_s, kn_s, vn_s, hid_s, qc_s, k_s, v_s, wloc, wall, tk, tv, sbuf, bias, caus,
    mrun, mfin, lrun, acc, heads, rs_in, rs_out, outb, crossb,
    lsem, kvsem, grecv, gsib, gsend, rrecv, rsend,
):
    me = lax.axis_index("req")
    z = lax.axis_index("tp")
    x, y, c = me // 8, (me // 2) % 4, me % 2
    d = 1 - 2 * c

    def rid(ax, ay, ac):
        return (((ax + 8) % 4) * 4 + (ay + 8) % 4) * 2 + ac

    sib = (rid(x, y, 1 - c), z)
    zp = (me, (z + 1) % 8)
    zm = (me, (z + 7) % 8)

    def shift(axis, by):
        if axis == "x":
            return (rid(x + by, y, c), z)
        return (rid(x, y + by, c), z)

    wcopy = pltpu.make_async_copy(w_h, wloc, lsem.at[0])
    wcopy.start()
    small = [
        pltpu.make_async_copy(src, dst, lsem.at[i])
        for i, (src, dst) in enumerate([(q_h, q_s), (kn_h, kn_s), (vn_h, vn_s), (hid_h, hid_s), (qc_h, qc_s)], 1)
    ]
    for cp in small[:3]:
        cp.start()

    def kv_copy(h):
        return (
            pltpu.make_async_copy(ck_h.at[0, :, pl.ds(h * HD, HD)], k_s.at[h], kvsem.at[0, h]),
            pltpu.make_async_copy(cv_h.at[0, :, pl.ds(h * HD, HD)], v_s.at[h], kvsem.at[1, h]),
        )

    kv = [kv_copy(h) for h in range(NH)]
    for kc, vc in kv:
        kc.start()
        vc.start()
    own_text = (
        pltpu.make_async_copy(tk_h, tk.at[me], lsem.at[6]),
        pltpu.make_async_copy(tv_h, tv.at[me], lsem.at[7]),
    )
    for cp in own_text:
        cp.start()
    for cp in small[3:]:
        cp.start()

    barrier = pltpu.get_barrier_semaphore()
    nbrs = (shift("x", 1), shift("x", -1), shift("y", 1), shift("y", -1), sib, zp, zm)
    for nb in nbrs:
        pl.semaphore_signal(barrier, inc=1, device_id=nb, device_id_type=MESH)

    wcopy.wait()
    mine = pl.multiple_of(me * 160, 32)
    wall[pl.ds(mine, 128), :] = wloc[:, 0:128].T
    wall[pl.ds(pl.multiple_of(mine + 128, 32), 32), :] = wloc[:, 128:160].T

    length = len_ref[me]
    col = lax.broadcasted_iota(jnp.int32, (8, CAP), 1)
    bias[...] = jnp.where(col < length, 0.0, NEG).astype(F32)
    ri = lax.broadcasted_iota(jnp.int32, (ROWS, ROWS), 0)
    ci = lax.broadcasted_iota(jnp.int32, (ROWS, ROWS), 1)
    caus[...] = jnp.where(ci <= ri, 0.0, NEG).astype(F32)

    def piece(p, ab, ax, ay, ac):
        r = rid(ax, ay, ac)
        if p == 0:
            return wall.at[pl.ds(pl.multiple_of(r * 160 + ab * 80, 16), 80)]
        return (tk if ab == 0 else tv).at[r]

    def some(p, ab, n):
        if p == 0:
            return wall.at[pl.ds(0, 80 * n)]
        return (tk if ab == 0 else tv).at[pl.ds(0, n)]

    class Gather:
        def __init__(self, p, ab):
            self.p, self.ab = p, ab
            self.f, self.g = ("y", "x") if ab == 0 else ("x", "y")

        def ref(self, rf, rg):
            if self.ab == 0:
                return piece(self.p, self.ab, x + rg, y + rf, c)
            return piece(self.p, self.ab, x + rf, y + rg, c)

        def copy(self, ref, dev, rf, rg):
            return pltpu.make_async_remote_copy(
                src_ref=ref, dst_ref=ref,
                send_sem=gsend.at[self.p, self.ab],
                recv_sem=grecv.at[self.p, self.ab, (rf % 4) * 4 + rg % 4],
                device_id=dev, device_id_type=MESH,
            )

        def to_f(self, rf, rg, by, nf):
            self.copy(self.ref(rf, rg), shift(self.f, by), nf, 0).start()

        def to_g(self, rf, rg, by, nf, ng):
            self.copy(self.ref(rf, rg), shift(self.g, by), nf, ng).start()

        def both_g(self, rf):
            for by in (1, -1):
                self.to_g(rf, 0, by, rf, -by)

        def to_sib(self, rf, rg):
            ref = self.ref(rf, rg)
            pltpu.make_async_remote_copy(
                src_ref=ref, dst_ref=ref,
                send_sem=gsend.at[self.p, self.ab],
                recv_sem=gsib.at[self.p, self.ab],
                device_id=sib, device_id_type=MESH,
            ).start()

        def wait(self, rf, rg):
            self.copy(self.ref(rf, rg), sib, rf, rg).wait_recv()

        def wait_sib(self):
            ref = some(self.p, self.ab, 16)
            pltpu.make_async_remote_copy(
                src_ref=ref, dst_ref=ref,
                send_sem=gsend.at[self.p, self.ab],
                recv_sem=gsib.at[self.p, self.ab],
                device_id=sib, device_id_type=MESH,
            ).wait_recv()

        def wait_send(self):
            self.copy(some(self.p, self.ab, 31), sib, 0, 0).wait_send()

    pairs = [(Gather(0, 0), Gather(0, 1)), (Gather(1, 0), Gather(1, 1))]

    def stage(p, n):
        gs = pairs[p]
        if n == 0:
            for g in gs:
                for by in (1, -1):
                    g.to_f(0, 0, by, -by)
            for g in gs:
                g.both_g(0)
            for g in gs:
                g.to_sib(0, 0)
        elif n == 1:
            for g in gs:
                g.wait(1, 0)
                g.wait(3, 0)
                g.to_f(-d, 0, d, 2)
                g.both_g(1)
                g.both_g(3)
            for g in gs:
                g.to_sib(1, 0)
                g.to_sib(3, 0)
        elif n == 2:
            for g in gs:
                g.wait(2, 0)
                g.both_g(2)
            for g in gs:
                g.wait(0, 1)
                g.wait(0, 3)
                g.to_g(0, -d, d, 0, 2)
            for g in gs:
                g.to_sib(2, 0)
                g.to_sib(0, 1)
                g.to_sib(0, 3)
        elif n == 3:
            for g in gs:
                for rf in (1, 3):
                    g.wait(rf, 1)
                    g.wait(rf, 3)
                    g.to_g(rf, -d, d, rf, 2)
            for g in gs:
                for rf in (1, 3):
                    g.to_sib(rf, 1)
                    g.to_sib(rf, 3)
        elif n == 4:
            for g in gs:
                g.wait(2, 1)
                g.wait(2, 3)
                g.to_g(2, -d, d, 2, 2)
                g.wait(0, 2)
            for g in gs:
                g.to_sib(2, 1)
                g.to_sib(2, 3)
                g.to_sib(0, 2)
        elif n == 5:
            for g in gs:
                for rf in (1, 3):
                    g.wait(rf, 2)
                    g.to_sib(rf, 2)
        elif n == 6:
            for g in gs:
                g.wait(2, 2)
                g.to_sib(2, 2)
        else:
            for g in gs:
                g.wait_sib()

    def qk_new(h):
        sl = slice(h * HD, (h + 1) * HD)
        s = lax.dot_general(q_s[:, sl], kn_s[:, sl], NT, preferred_element_type=F32)
        s = s + caus[...]
        sbuf[h % 2, :, CAP:KEYS] = s
        mrun[...] = jnp.maximum(s[:, 0:128], s[:, 128:256])

    def qk_chunk(h, i):
        sl = slice(h * HD, (h + 1) * HD)
        at = pl.multiple_of(i * CHUNK, CHUNK)
        s = lax.dot_general(q_s[:, sl], k_s[h, pl.ds(at, CHUNK), :], NT, preferred_element_type=F32)
        s = s + bias[0:1, pl.ds(at, CHUNK)]
        sbuf[h % 2, :, pl.ds(at, CHUNK)] = s
        m = jnp.maximum(jnp.maximum(s[:, 0:128], s[:, 128:256]), jnp.maximum(s[:, 256:384], s[:, 384:512]))
        mrun[...] = jnp.maximum(mrun[...], m)

    def set_max():
        mfin[...] = jnp.broadcast_to(jnp.max(mrun[...], axis=1, keepdims=True), (ROWS, HD))

    def pv(p, v, lane_tiles):
        part = p[:, 0:128]
        for t in range(1, lane_tiles):
            part = part + p[:, t * 128:(t + 1) * 128]
        return part, jnp.dot(p.astype(BF16), v, preferred_element_type=F32)

    def weigh(s, lane_tiles):
        m = mfin[...]
        return jnp.concatenate(
            [jnp.exp2((s[:, t * 128:(t + 1) * 128] - m) * (SCALE * LOG2E)) for t in range(lane_tiles)], axis=1
        )

    def pv_new(h):
        sl = slice(h * HD, (h + 1) * HD)
        p = weigh(sbuf[h % 2, :, CAP:KEYS], 2)
        part, o = pv(p, vn_s[:, sl], 2)
        lrun[...] = part
        acc[...] = o

    def pv_chunk(h, i):
        at = pl.multiple_of(i * CHUNK, CHUNK)
        p = weigh(sbuf[h % 2, :, pl.ds(at, CHUNK)], 4)
        part, o = pv(p, v_s[h, pl.ds(at, CHUNK), :], 4)
        lrun[...] += part
        acc[...] += o

    def head_stage(h):
        if h < NH:
            kv[h][0].wait()
        if h > 0:
            kv[h - 1][1].wait()
            pv_new(h - 1)
        if h < NH:
            qk_new(h)

        @pl.loop(0, CAP // CHUNK)
        def _(i):
            if h < NH:
                qk_chunk(h, i)
            if h > 0:
                pv_chunk(h - 1, i)

        if h > 0:
            mass = jnp.sum(lrun[...], axis=1, keepdims=True)
            heads[:, (h - 1) * HD:h * HD] = (acc[...] / mass).astype(BF16)
        if h < NH:
            set_max()

    prompt = prompt_ref[0]

    def cross_head(h):
        sl = slice(h * HD, (h + 1) * HD)
        kt = tk[:, prompt, :, sl].reshape(512, HD)
        vt = tv[:, prompt, :, sl].reshape(512, HD)
        s = lax.dot_general(qc_s[:, sl], kt, NT, preferred_element_type=F32)
        m = jnp.max(s, axis=1, keepdims=True)
        p = jnp.exp2((s - m) * (SCALE * LOG2E))
        mass = jnp.sum(p, axis=1, keepdims=True)
        o = jnp.dot(p.astype(BF16), vt, preferred_element_type=F32)
        crossb[:, sl] = (o / mass).astype(BF16)

    groups = ((0, 3), (3, 2))

    def term(g, s):
        first, count = groups[g]
        way = d if g == 0 else -d
        b = (z - way * (1 + s) + 16) % 8
        at = pl.multiple_of(b * W + first * HD, HD)
        wt = wall[pl.ds(at, count * HD), :]
        return lax.dot_general(heads[...], wt, NT, preferred_element_type=F32)

    def rs_copy(g, j, s):
        way = d if g == 0 else -d
        return pltpu.make_async_remote_copy(
            src_ref=rs_out.at[j, s], dst_ref=rs_in.at[j, s],
            send_sem=rsend.at[j, s], recv_sem=rrecv.at[j, s],
            device_id=(me, (z + way + 8) % 8), device_id_type=MESH,
        )

    def rs_first():
        for g, (first, count) in enumerate(groups):
            t = term(g, 0)
            for k in range(count):
                rs_out[first + k, 0] = t[:, k * HD:(k + 1) * HD].astype(BF16)
            for k in range(count):
                rs_copy(g, first + k, 0).start()

    def rs_step(s):
        for g, (first, count) in enumerate(groups):
            t = term(g, s + 1)
            for k in range(count):
                j = first + k
                rs_copy(g, j, s).wait_recv()
                total = rs_in[j, s].astype(F32) + t[:, k * HD:(k + 1) * HD]
                if s < 6:
                    rs_out[j, s + 1] = total.astype(BF16)
                    rs_copy(g, j, s + 1).start()
                else:
                    sl = slice(j * HD, (j + 1) * HD)
                    outb[:, sl] = (hid_s[:, sl].astype(F32) + total).astype(BF16)

    pl.semaphore_wait(barrier, len(nbrs))
    stage(0, 0)
    for cp in small[:3]:
        cp.wait()
    head_stage(0)
    head_stage(1)
    stage(0, 1)
    head_stage(2)
    head_stage(3)
    stage(0, 2)
    head_stage(4)
    stage(0, 3)
    head_stage(5)
    for cp in own_text:
        cp.wait()
    stage(0, 4)
    stage(1, 0)
    stage(0, 5)
    stage(0, 6)
    stage(0, 7)
    rs_first()
    for cp in small[3:]:
        cp.wait()
    rs_step(0)
    stage(1, 1)
    rs_step(1)
    stage(1, 2)
    rs_step(2)
    stage(1, 3)
    rs_step(3)
    stage(1, 4)
    rs_step(4)
    stage(1, 5)
    stage(1, 6)
    stage(1, 7)
    cross_head(0)
    cross_head(1)
    cross_head(2)
    rs_step(5)
    cross_head(3)
    cross_head(4)
    cross_out = pltpu.make_async_copy(crossb, cross_h, lsem.at[8])
    cross_out.start()
    rs_step(6)
    hid_out = pltpu.make_async_copy(outb, out_h, lsem.at[9])
    hid_out.start()
    for ps in pairs:
        for g in ps:
            g.wait_send()
    for g, (first, count) in enumerate(groups):
        for k in range(count):
            for s in range(7):
                rs_copy(g, first + k, s).wait_send()
    cross_out.wait()
    hid_out.wait()


def per_device(
    hidden, q_new, k_new, v_new, cache_k, cache_v, cache_len, w_out, q_cross, text_k, text_v, prompt_of,
):
    any_spec = pl.BlockSpec(memory_space=pl.ANY)
    smem = pl.BlockSpec(memory_space=pltpu.SMEM)
    v = pltpu.VMEM
    dma = pltpu.SemaphoreType.DMA
    return pl.pallas_call(
        kernel,
        out_shape=(
            jax.ShapeDtypeStruct((ROWS, W), BF16),
            jax.ShapeDtypeStruct((ROWS, W), BF16),
        ),
        in_specs=[smem, smem] + [any_spec] * 10,
        out_specs=(any_spec, any_spec),
        scratch_shapes=[
            v((ROWS, W), BF16), v((ROWS, W), BF16), v((ROWS, W), BF16), v((ROWS, W), BF16), v((ROWS, W), BF16),
            v((NH, CAP, HD), BF16), v((NH, CAP, HD), BF16),
            v((W, 160), BF16), v((8 * W, W), BF16),
            v((32, 4, 16, W), BF16), v((32, 4, 16, W), BF16),
            v((2, ROWS, KEYS), F32), v((8, CAP), F32), v((ROWS, ROWS), F32),
            v((ROWS, HD), F32), v((ROWS, HD), F32), v((ROWS, HD), F32), v((ROWS, HD), F32),
            v((ROWS, W), BF16),
            v((NH, 7, ROWS, HD), BF16), v((NH, 7, ROWS, HD), BF16),
            v((ROWS, W), BF16), v((ROWS, W), BF16),
            dma((10,)), dma((2, NH)), dma((2, 2, 16)), dma((2, 2)), dma((2, 2)), dma((NH, 7)), dma((NH, 7)),
        ],
        compiler_params=pltpu.CompilerParams(
            collective_id=0, has_side_effects=True, vmem_limit_bytes=60 * 1024 * 1024
        ),
    )(cache_len, prompt_of, hidden, q_new, k_new, v_new, cache_k, cache_v, w_out, q_cross, text_k, text_v)


def solution(mesh):
    placed = (
        P("req", "tp"), P("req", "tp"), P("req", "tp"), P("req", "tp"),
        P("req", None, "tp"), P("req", None, "tp"),
        P(), P("tp", "req"), P("req", "tp"),
        P(None, "req", "tp"), P(None, "req", "tp"), P("req"),
    )
    return jax.shard_map(
        per_device,
        mesh=mesh,
        in_specs=placed,
        out_specs=(P("req", "tp"), P("req", "tp")),
        check_vma=False,
    )
```

```python
import jax
import jax.numpy as jnp
from jax import lax
from jax.experimental import pallas as pl
from jax.experimental.pallas import tpu as pltpu
from jax.sharding import PartitionSpec as P

MESH = pl.DeviceIdType.MESH
HD = 128
NH = 5
ROWS = 256
W = NH * HD
CAP = 4096
KEYS = CAP + ROWS
CHUNK = 1024
TILES = CHUNK // HD
TURN = 160
NEG = -1e30
SCALE = HD**-0.5
LOG2E = 1.4426950408889634
NT = (((1,), (1,)), ((), ()))
F32 = jnp.float32
BF16 = jnp.bfloat16


def kernel(
    len_ref, prompt_ref, hid_h, q_h, kn_h, vn_h, ck_h, cv_h, w_h, qc_h, tk_h, tv_h,
    outb, crossb,
    q_s, kn_s, vn_s, hid_s, qc_s, k_s, v_s, wall, tk, tv, sbuf, bias, caus,
    mrun, mfin, lrun, acc, heads, outt, rs_in, rs_out,
    lsem, kvsem, grecv, gsib, gsend, rrecv, rsend,
):
    me = lax.axis_index("req")
    z = lax.axis_index("tp")
    x, y, c = me // 8, (me // 2) % 4, me % 2
    d = 1 - 2 * c

    def rid(ax, ay, ac):
        return (((ax + 8) % 4) * 4 + (ay + 8) % 4) * 2 + ac

    sib = (rid(x, y, 1 - c), z)
    zp = (me, (z + 1) % 8)
    zm = (me, (z + 7) % 8)

    def shift(axis, by):
        if axis == "x":
            return (rid(x + by, y, c), z)
        return (rid(x, y + by, c), z)

    mine = pl.multiple_of(me * 160, 32)
    wcopy = pltpu.make_async_copy(w_h, wall.at[pl.ds(mine, 160)], lsem.at[0])
    wcopy.start()
    small = [
        pltpu.make_async_copy(src, dst, lsem.at[i])
        for i, (src, dst) in enumerate([(q_h, q_s), (kn_h, kn_s), (vn_h, vn_s), (hid_h, hid_s), (qc_h, qc_s)], 1)
    ]
    for cp in small[:3]:
        cp.start()

    def kv_copy(h):
        return (
            pltpu.make_async_copy(ck_h.at[0, :, pl.ds(h * HD, HD)], k_s.at[h], kvsem.at[0, h]),
            pltpu.make_async_copy(cv_h.at[0, :, pl.ds(h * HD, HD)], v_s.at[h], kvsem.at[1, h]),
        )

    kv = [kv_copy(h) for h in range(NH)]
    for kc, vc in kv:
        kc.start()
        vc.start()
    own_text = (
        pltpu.make_async_copy(tk_h, tk.at[me], lsem.at[6]),
        pltpu.make_async_copy(tv_h, tv.at[me], lsem.at[7]),
    )
    for cp in own_text:
        cp.start()
    for cp in small[3:]:
        cp.start()

    barrier = pltpu.get_barrier_semaphore()
    nbrs = (shift("x", 1), shift("x", -1), shift("y", 1), shift("y", -1), sib, zp, zm)
    for nb in nbrs:
        pl.semaphore_signal(barrier, inc=1, device_id=nb, device_id_type=MESH)

    def piece(p, ab, ax, ay, ac):
        r = rid(ax, ay, ac)
        if p == 0:
            return wall.at[pl.ds(pl.multiple_of(r * 160 + ab * 80, 16), 80)]
        return (tk if ab == 0 else tv).at[r]

    def some(p, ab, n):
        if p == 0:
            return wall.at[pl.ds(0, 80 * n)]
        return (tk if ab == 0 else tv).at[pl.ds(0, n)]

    class Gather:
        def __init__(self, p, ab):
            self.p, self.ab = p, ab
            self.f, self.g = ("y", "x") if ab == 0 else ("x", "y")

        def ref(self, rf, rg):
            if self.ab == 0:
                return piece(self.p, self.ab, x + rg, y + rf, c)
            return piece(self.p, self.ab, x + rf, y + rg, c)

        def copy(self, ref, dev, rf, rg):
            return pltpu.make_async_remote_copy(
                src_ref=ref, dst_ref=ref,
                send_sem=gsend.at[self.p, self.ab],
                recv_sem=grecv.at[self.p, self.ab, (rf % 4) * 4 + rg % 4],
                device_id=dev, device_id_type=MESH,
            )

        def to_f(self, rf, rg, by, nf):
            self.copy(self.ref(rf, rg), shift(self.f, by), nf, 0).start()

        def to_g(self, rf, rg, by, nf, ng):
            self.copy(self.ref(rf, rg), shift(self.g, by), nf, ng).start()

        def both_g(self, rf):
            for by in (1, -1):
                self.to_g(rf, 0, by, rf, -by)

        def to_sib(self, rf, rg):
            ref = self.ref(rf, rg)
            pltpu.make_async_remote_copy(
                src_ref=ref, dst_ref=ref,
                send_sem=gsend.at[self.p, self.ab],
                recv_sem=gsib.at[self.p, self.ab],
                device_id=sib, device_id_type=MESH,
            ).start()

        def wait(self, rf, rg):
            self.copy(self.ref(rf, rg), sib, rf, rg).wait_recv()

        def wait_sib(self):
            ref = some(self.p, self.ab, 16)
            pltpu.make_async_remote_copy(
                src_ref=ref, dst_ref=ref,
                send_sem=gsend.at[self.p, self.ab],
                recv_sem=gsib.at[self.p, self.ab],
                device_id=sib, device_id_type=MESH,
            ).wait_recv()

        def wait_send(self):
            self.copy(some(self.p, self.ab, 31), sib, 0, 0).wait_send()

    pairs = [(Gather(0, 0), Gather(0, 1)), (Gather(1, 0), Gather(1, 1))]

    def stage(p, n):
        gs = pairs[p]
        if n == 0:
            for g in gs:
                for by in (1, -1):
                    g.to_f(0, 0, by, -by)
            for g in gs:
                g.both_g(0)
            for g in gs:
                g.to_sib(0, 0)
        elif n == 1:
            for g in gs:
                g.wait(1, 0)
                g.wait(3, 0)
                g.to_f(-d, 0, d, 2)
            for g in gs:
                g.both_g(1)
                g.both_g(3)
            for g in gs:
                g.to_sib(1, 0)
                g.to_sib(3, 0)
        elif n == 2:
            for g in gs:
                g.wait(2, 0)
                g.both_g(2)
            for g in gs:
                g.to_sib(2, 0)
        elif n == 3:
            for g in gs:
                for rf in (1, 3):
                    g.wait(rf, 1)
                    g.wait(rf, 3)
                    g.to_g(rf, -d, d, rf, 2)
            for g in gs:
                for rf in (1, 3):
                    g.to_sib(rf, 1)
                    g.to_sib(rf, 3)
        elif n == 4:
            for g in gs:
                g.wait(2, 1)
                g.wait(2, 3)
                g.to_g(2, -d, d, 2, 2)
            for g in gs:
                g.to_sib(2, 1)
                g.to_sib(2, 3)
        elif n == 5:
            for g in gs:
                g.wait(0, 1)
                g.wait(0, 3)
                g.to_g(0, -d, d, 0, 2)
            for g in gs:
                g.to_sib(0, 1)
                g.to_sib(0, 3)
            for g in gs:
                for rf in (1, 3):
                    g.wait(rf, 2)
                    g.to_sib(rf, 2)
        elif n == 6:
            for g in gs:
                g.wait(2, 2)
                g.wait(0, 2)
            for g in gs:
                g.to_sib(2, 2)
                g.to_sib(0, 2)
        else:
            for g in gs:
                g.wait_sib()

    def qk_new(h):
        sl = slice(h * HD, (h + 1) * HD)
        s = lax.dot_general(q_s[:, sl], kn_s[:, sl], NT, preferred_element_type=F32)
        s = s + caus[...]
        sbuf[h % 2, :, CAP:KEYS] = s
        mrun[...] = jnp.maximum(s[:, 0:128], s[:, 128:256])

    def qk_chunk(h, i):
        sl = slice(h * HD, (h + 1) * HD)
        at = pl.multiple_of(i * CHUNK, CHUNK)
        s = lax.dot_general(q_s[:, sl], k_s[h, pl.ds(at, CHUNK), :], NT, preferred_element_type=F32)
        s = s + bias[0:1, pl.ds(at, CHUNK)]
        sbuf[h % 2, :, pl.ds(at, CHUNK)] = s
        m = mrun[...]
        for t in range(TILES):
            m = jnp.maximum(m, s[:, t * HD:(t + 1) * HD])
        mrun[...] = m

    def set_max():
        mfin[...] = jnp.broadcast_to(jnp.max(mrun[...], axis=1, keepdims=True), (ROWS, HD))

    def pv(p, v, lane_tiles):
        part = p[:, 0:128]
        for t in range(1, lane_tiles):
            part = part + p[:, t * 128:(t + 1) * 128]
        return part, jnp.dot(p.astype(BF16), v, preferred_element_type=F32)

    def weigh(s, lane_tiles):
        m = mfin[...]
        return jnp.concatenate(
            [jnp.exp2((s[:, t * 128:(t + 1) * 128] - m) * (SCALE * LOG2E)) for t in range(lane_tiles)], axis=1
        )

    def pv_new(h):
        sl = slice(h * HD, (h + 1) * HD)
        p = weigh(sbuf[h % 2, :, CAP:KEYS], 2)
        part, o = pv(p, vn_s[:, sl], 2)
        lrun[...] = part
        acc[...] = o

    def pv_chunk(h, i):
        at = pl.multiple_of(i * CHUNK, CHUNK)
        p = weigh(sbuf[h % 2, :, pl.ds(at, CHUNK)], TILES)
        part, o = pv(p, v_s[h, pl.ds(at, CHUNK), :], TILES)
        lrun[...] += part
        acc[...] += o

    def head_stage(h):
        if h < NH:
            kv[h][0].wait()
        if h > 0:
            kv[h - 1][1].wait()
            pv_new(h - 1)
        if h < NH:
            qk_new(h)

        @pl.loop(0, CAP // CHUNK)
        def _(i):
            if h < NH:
                qk_chunk(h, i)
            if h > 0:
                pv_chunk(h - 1, i)

        if h > 0:
            mass = jnp.sum(lrun[...], axis=1, keepdims=True)
            heads[:, (h - 1) * HD:h * HD] = (acc[...] / mass).astype(BF16)
        if h < NH:
            set_max()

    prompt = prompt_ref[0]

    def cross_head(h):
        sl = slice(h * HD, (h + 1) * HD)
        kt = tk[:, prompt, :, sl].reshape(512, HD)
        vt = tv[:, prompt, :, sl].reshape(512, HD)
        s = lax.dot_general(qc_s[:, sl], kt, NT, preferred_element_type=F32)
        m = jnp.max(s, axis=1, keepdims=True)
        p = jnp.exp2((s - m) * (SCALE * LOG2E))
        mass = jnp.sum(p, axis=1, keepdims=True)
        o = jnp.dot(p.astype(BF16), vt, preferred_element_type=F32)
        crossb[:, sl] = (o / mass).astype(BF16)

    flows = ((d, 4), (-d, 3))
    PARTS = W // TURN

    def term(b, k):
        at = pl.multiple_of(b * W + k * TURN, 32)
        return lax.dot_general(wall[pl.ds(at, TURN), :], heads[...], NT, preferred_element_type=F32)

    def rs_copy(f, s, k):
        way = flows[f][0]
        return pltpu.make_async_remote_copy(
            src_ref=rs_out.at[f, s, k], dst_ref=rs_in.at[f, s, k],
            send_sem=rsend.at[f, s, k], recv_sem=rrecv.at[f, s, k],
            device_id=(me, (z + way + 8) % 8), device_id_type=MESH,
        )

    def rs_block(f, s):
        way, hops = flows[f]
        return (z + (hops - s) * way + 8) % 8

    def rs_first():
        for k in range(PARTS):
            for f in range(2):
                rs_out[f, 0, k] = term(rs_block(f, 0), k).astype(BF16)
                rs_copy(f, 0, k).start()

    def rs_step(s):
        for k in range(PARTS):
            for f in range(2):
                if s < flows[f][1]:
                    t = term(rs_block(f, s), k)
                    rs_copy(f, s - 1, k).wait_recv()
                    rs_out[f, s, k] = (rs_in[f, s - 1, k].astype(F32) + t).astype(BF16)
                    rs_copy(f, s, k).start()

    def rs_own():
        for k in range(PARTS):
            t = term(z, k)
            rs_copy(1, 2, k).wait_recv()
            outt[k * TURN:(k + 1) * TURN, :] = t + rs_in[1, 2, k].astype(F32)

    def rs_last():
        for k in range(PARTS):
            rs_copy(0, 3, k).wait_recv()
            at = slice(k * TURN, (k + 1) * TURN)
            outt[at, :] = outt[at, :] + rs_in[0, 3, k].astype(F32)
        for j in range(NH):
            sl = slice(j * HD, (j + 1) * HD)
            outb[:, sl] = (hid_s[:, sl].astype(F32) + outt[sl, :].T).astype(BF16)

    def masks():
        length = len_ref[me]
        col = lax.broadcasted_iota(jnp.int32, (8, CAP), 1)
        bias[...] = jnp.where(col < length, 0.0, NEG).astype(F32)
        ri = lax.broadcasted_iota(jnp.int32, (ROWS, ROWS), 0)
        ci = lax.broadcasted_iota(jnp.int32, (ROWS, ROWS), 1)
        caus[...] = jnp.where(ci <= ri, 0.0, NEG).astype(F32)

    wcopy.wait()
    pl.semaphore_wait(barrier, len(nbrs))
    stage(0, 0)
    masks()
    for cp in small[:3]:
        cp.wait()
    head_stage(0)
    head_stage(1)
    stage(0, 1)
    head_stage(2)
    head_stage(3)
    stage(0, 2)
    head_stage(4)
    stage(0, 3)
    head_stage(5)
    stage(0, 4)
    for cp in own_text:
        cp.wait()
    stage(0, 5)
    stage(1, 0)
    stage(0, 6)
    stage(0, 7)
    rs_first()
    for cp in small[3:]:
        cp.wait()
    stage(1, 1)
    rs_step(1)
    stage(1, 2)
    stage(1, 3)
    rs_step(2)
    stage(1, 4)
    stage(1, 5)
    stage(1, 6)
    rs_step(3)
    stage(1, 7)
    rs_own()
    for h in range(NH):
        cross_head(h)
    rs_last()
    for ps in pairs:
        for g in ps:
            g.wait_send()
    for k in range(PARTS):
        for f in range(2):
            for s in range(flows[f][1]):
                rs_copy(f, s, k).wait_send()


def per_device(
    hidden, q_new, k_new, v_new, cache_k, cache_v, cache_len, w_out, q_cross, text_k, text_v, prompt_of,
):
    any_spec = pl.BlockSpec(memory_space=pl.ANY)
    smem = pl.BlockSpec(memory_space=pltpu.SMEM)
    v = pltpu.VMEM
    dma = pltpu.SemaphoreType.DMA
    vmem = pl.BlockSpec(memory_space=pltpu.VMEM)
    return pl.pallas_call(
        kernel,
        out_shape=(v((ROWS, W), BF16), v((ROWS, W), BF16)),
        in_specs=[smem, smem] + [any_spec] * 10,
        out_specs=(vmem, vmem),
        scratch_shapes=[
            v((ROWS, W), BF16), v((ROWS, W), BF16), v((ROWS, W), BF16), v((ROWS, W), BF16), v((ROWS, W), BF16),
            v((NH, CAP, HD), BF16), v((NH, CAP, HD), BF16),
            v((8 * W, W), BF16),
            v((32, 4, 16, W), BF16), v((32, 4, 16, W), BF16),
            v((2, ROWS, KEYS), F32), v((8, CAP), F32), v((ROWS, ROWS), F32),
            v((ROWS, HD), F32), v((ROWS, HD), F32), v((ROWS, HD), F32), v((ROWS, HD), F32),
            v((ROWS, W), BF16), v((W, ROWS), F32),
            v((2, 4, 4, TURN, ROWS), BF16), v((2, 4, 4, TURN, ROWS), BF16),
            dma((8,)), dma((2, NH)), dma((2, 2, 16)), dma((2, 2)), dma((2, 2)), dma((2, 4, 4)), dma((2, 4, 4)),
        ],
        compiler_params=pltpu.CompilerParams(
            collective_id=0, has_side_effects=True, vmem_limit_bytes=56 * 1024 * 1024
        ),
    )(cache_len, prompt_of, hidden, q_new, k_new, v_new, cache_k, cache_v, w_out.T, q_cross, text_k, text_v)


def solution(mesh):
    placed = (
        P("req", "tp"), P("req", "tp"), P("req", "tp"), P("req", "tp"),
        P("req", None, "tp"), P("req", None, "tp"),
        P(), P("tp", "req"), P("req", "tp"),
        P(None, "req", "tp"), P(None, "req", "tp"), P("req"),
    )
    return jax.shard_map(
        per_device,
        mesh=mesh,
        in_specs=placed,
        out_specs=(P("req", "tp"), P("req", "tp")),
        check_vma=False,
    )
```

```python
import jax
import jax.numpy as jnp
from jax import lax
from jax.experimental import pallas as pl
from jax.experimental.pallas import tpu as pltpu
from jax.sharding import PartitionSpec as P

MESH = pl.DeviceIdType.MESH
HD = 128
NH = 5
ROWS = 256
W = NH * HD
CAP = 4096
KEYS = CAP + ROWS
CHUNK = 1024
TILES = CHUNK // HD
HALVES = (48, 32)
PART = 128
NEG = -1e30
SCALE = HD**-0.5
LOG2E = 1.4426950408889634
NT = (((1,), (1,)), ((), ()))
F32 = jnp.float32
BF16 = jnp.bfloat16


def kernel(
    len_ref, prompt_ref, hid_h, q_h, kn_h, vn_h, ck_h, cv_h, w_h, qc_h, tk_h, tv_h,
    outb, crossb,
    q_s, kn_s, vn_s, hid_s, qc_s, k_s, v_s, wall0, wall1, tk, tv, sbuf, bias, caus,
    mrun, mfin, lrun, acc, heads, outt, rs_in, rs_out,
    lsem, kvsem, grecv, gsib, gsend, rrecv, rsend,
):
    me = lax.axis_index("req")
    z = lax.axis_index("tp")
    x, y, c = me // 8, (me // 2) % 4, me % 2
    d = 1 - 2 * c

    def rid(ax, ay, ac):
        return (((ax + 8) % 4) * 4 + (ay + 8) % 4) * 2 + ac

    sib = (rid(x, y, 1 - c), z)
    zp = (me, (z + 1) % 8)
    zm = (me, (z + 7) % 8)

    def shift(axis, by):
        if axis == "x":
            return (rid(x + by, y, c), z)
        return (rid(x, y + by, c), z)

    walls = (wall0, wall1)

    def own_rows(p):
        n = 2 * HALVES[p]
        return walls[p].at[pl.ds(pl.multiple_of(me * n, n), n)]

    wcopies = (
        pltpu.make_async_copy(w_h.at[pl.ds(0, 96)], own_rows(0), lsem.at[0]),
        pltpu.make_async_copy(w_h.at[pl.ds(96, 64)], own_rows(1), lsem.at[8]),
    )
    for cp in wcopies:
        cp.start()
    small = [
        pltpu.make_async_copy(src, dst, lsem.at[i])
        for i, (src, dst) in enumerate([(q_h, q_s), (kn_h, kn_s), (vn_h, vn_s), (hid_h, hid_s), (qc_h, qc_s)], 1)
    ]
    for cp in small[:3]:
        cp.start()

    def kv_copy(h):
        return (
            pltpu.make_async_copy(ck_h.at[0, :, pl.ds(h * HD, HD)], k_s.at[h], kvsem.at[0, h]),
            pltpu.make_async_copy(cv_h.at[0, :, pl.ds(h * HD, HD)], v_s.at[h], kvsem.at[1, h]),
        )

    kv = [kv_copy(h) for h in range(NH)]
    for kc, vc in kv:
        kc.start()
        vc.start()
    own_text = (
        pltpu.make_async_copy(tk_h, tk.at[me], lsem.at[6]),
        pltpu.make_async_copy(tv_h, tv.at[me], lsem.at[7]),
    )
    for cp in own_text:
        cp.start()
    for cp in small[3:]:
        cp.start()

    barrier = pltpu.get_barrier_semaphore()
    nbrs = (shift("x", 1), shift("x", -1), shift("y", 1), shift("y", -1), sib, zp, zm)
    for nb in nbrs:
        pl.semaphore_signal(barrier, inc=1, device_id=nb, device_id_type=MESH)

    def piece(p, ab, ax, ay, ac):
        r = rid(ax, ay, ac)
        if p < 2:
            n = HALVES[p]
            return walls[p].at[pl.ds(pl.multiple_of(r * 2 * n + ab * n, n), n)]
        return (tk if ab == 0 else tv).at[r]

    def some(p, ab, n):
        if p < 2:
            return walls[p].at[pl.ds(0, HALVES[p] * n)]
        return (tk if ab == 0 else tv).at[pl.ds(0, n)]

    class Gather:
        def __init__(self, p, ab):
            self.p, self.ab = p, ab
            self.f, self.g = ("y", "x") if ab == 0 else ("x", "y")

        def ref(self, rf, rg):
            if self.ab == 0:
                return piece(self.p, self.ab, x + rg, y + rf, c)
            return piece(self.p, self.ab, x + rf, y + rg, c)

        def copy(self, ref, dev, rf, rg):
            return pltpu.make_async_remote_copy(
                src_ref=ref, dst_ref=ref,
                send_sem=gsend.at[self.p, self.ab],
                recv_sem=grecv.at[self.p, self.ab, (rf % 4) * 4 + rg % 4],
                device_id=dev, device_id_type=MESH,
            )

        def to_f(self, rf, rg, by, nf):
            self.copy(self.ref(rf, rg), shift(self.f, by), nf, 0).start()

        def to_g(self, rf, rg, by, nf, ng):
            self.copy(self.ref(rf, rg), shift(self.g, by), nf, ng).start()

        def both_g(self, rf):
            for by in (1, -1):
                self.to_g(rf, 0, by, rf, -by)

        def to_sib(self, rf, rg):
            ref = self.ref(rf, rg)
            pltpu.make_async_remote_copy(
                src_ref=ref, dst_ref=ref,
                send_sem=gsend.at[self.p, self.ab],
                recv_sem=gsib.at[self.p, self.ab],
                device_id=sib, device_id_type=MESH,
            ).start()

        def wait(self, rf, rg):
            self.copy(self.ref(rf, rg), sib, rf, rg).wait_recv()

        def wait_sib(self):
            ref = some(self.p, self.ab, 16)
            pltpu.make_async_remote_copy(
                src_ref=ref, dst_ref=ref,
                send_sem=gsend.at[self.p, self.ab],
                recv_sem=gsib.at[self.p, self.ab],
                device_id=sib, device_id_type=MESH,
            ).wait_recv()

        def wait_send(self):
            self.copy(some(self.p, self.ab, 31), sib, 0, 0).wait_send()

    pairs = [(Gather(p, 0), Gather(p, 1)) for p in range(3)]

    def stage(p, n):
        gs = pairs[p]
        if n == 0:
            for g in gs:
                for by in (1, -1):
                    g.to_f(0, 0, by, -by)
            for g in gs:
                g.both_g(0)
            for g in gs:
                g.to_sib(0, 0)
        elif n == 1:
            for g in gs:
                g.wait(1, 0)
                g.wait(3, 0)
                g.to_f(-d, 0, d, 2)
            for g in gs:
                g.both_g(1)
                g.both_g(3)
            for g in gs:
                g.to_sib(1, 0)
                g.to_sib(3, 0)
        elif n == 2:
            for g in gs:
                g.wait(2, 0)
                g.both_g(2)
            for g in gs:
                g.to_sib(2, 0)
        elif n == 3:
            for g in gs:
                for rf in (1, 3):
                    g.wait(rf, 1)
                    g.wait(rf, 3)
                    g.to_g(rf, -d, d, rf, 2)
            for g in gs:
                for rf in (1, 3):
                    g.to_sib(rf, 1)
                    g.to_sib(rf, 3)
        elif n == 4:
            for g in gs:
                g.wait(2, 1)
                g.wait(2, 3)
                g.to_g(2, -d, d, 2, 2)
            for g in gs:
                g.to_sib(2, 1)
                g.to_sib(2, 3)
        elif n == 5:
            for g in gs:
                g.wait(0, 1)
                g.wait(0, 3)
                g.to_g(0, -d, d, 0, 2)
            for g in gs:
                g.to_sib(0, 1)
                g.to_sib(0, 3)
            for g in gs:
                for rf in (1, 3):
                    g.wait(rf, 2)
                    g.to_sib(rf, 2)
        elif n == 6:
            for g in gs:
                g.wait(2, 2)
                g.wait(0, 2)
            for g in gs:
                g.to_sib(2, 2)
                g.to_sib(0, 2)
        else:
            for g in gs:
                g.wait_sib()

    def qk_new(h):
        sl = slice(h * HD, (h + 1) * HD)
        s = lax.dot_general(q_s[:, sl], kn_s[:, sl], NT, preferred_element_type=F32)
        s = s + caus[...]
        sbuf[h % 2, :, CAP:KEYS] = s
        mrun[...] = jnp.maximum(s[:, 0:128], s[:, 128:256])

    def qk_chunk(h, i):
        sl = slice(h * HD, (h + 1) * HD)
        at = pl.multiple_of(i * CHUNK, CHUNK)
        s = lax.dot_general(q_s[:, sl], k_s[h, pl.ds(at, CHUNK), :], NT, preferred_element_type=F32)
        s = s + bias[0:1, pl.ds(at, CHUNK)]
        sbuf[h % 2, :, pl.ds(at, CHUNK)] = s
        m = mrun[...]
        for t in range(TILES):
            m = jnp.maximum(m, s[:, t * HD:(t + 1) * HD])
        mrun[...] = m

    def set_max():
        mfin[...] = jnp.broadcast_to(jnp.max(mrun[...], axis=1, keepdims=True), (ROWS, HD))

    def pv(p, v, lane_tiles):
        part = p[:, 0:128]
        for t in range(1, lane_tiles):
            part = part + p[:, t * 128:(t + 1) * 128]
        return part, jnp.dot(p.astype(BF16), v, preferred_element_type=F32)

    def weigh(s, lane_tiles):
        m = mfin[...]
        return jnp.concatenate(
            [jnp.exp2((s[:, t * 128:(t + 1) * 128] - m) * (SCALE * LOG2E)) for t in range(lane_tiles)], axis=1
        )

    def pv_new(h):
        sl = slice(h * HD, (h + 1) * HD)
        p = weigh(sbuf[h % 2, :, CAP:KEYS], 2)
        part, o = pv(p, vn_s[:, sl], 2)
        lrun[...] = part
        acc[...] = o

    def pv_chunk(h, i):
        at = pl.multiple_of(i * CHUNK, CHUNK)
        p = weigh(sbuf[h % 2, :, pl.ds(at, CHUNK)], TILES)
        part, o = pv(p, v_s[h, pl.ds(at, CHUNK), :], TILES)
        lrun[...] += part
        acc[...] += o

    def head_stage(h):
        if h < NH:
            kv[h][0].wait()
        if h > 0:
            kv[h - 1][1].wait()
            pv_new(h - 1)
        if h < NH:
            qk_new(h)

        @pl.loop(0, CAP // CHUNK)
        def _(i):
            if h < NH:
                qk_chunk(h, i)
            if h > 0:
                pv_chunk(h - 1, i)

        if h > 0:
            mass = jnp.sum(lrun[...], axis=1, keepdims=True)
            heads[:, (h - 1) * HD:h * HD] = (acc[...] / mass).astype(BF16)
        if h < NH:
            set_max()

    prompt = prompt_ref[0]

    def cross_head(h):
        sl = slice(h * HD, (h + 1) * HD)
        kt = tk[:, prompt, :, sl].reshape(512, HD)
        vt = tv[:, prompt, :, sl].reshape(512, HD)
        s = lax.dot_general(qc_s[:, sl], kt, NT, preferred_element_type=F32)
        m = jnp.max(s, axis=1, keepdims=True)
        p = jnp.exp2((s - m) * (SCALE * LOG2E))
        mass = jnp.sum(p, axis=1, keepdims=True)
        o = jnp.dot(p.astype(BF16), vt, preferred_element_type=F32)
        crossb[:, sl] = (o / mass).astype(BF16)

    flows = ((d, 4), (-d, 3))
    parts = ((0, 1, 2), (3, 4))

    def term(b, p):
        n = 8 * HALVES[p]
        wt = walls[p][pl.ds(pl.multiple_of(b * n, n), n), :]
        return lax.dot_general(wt, heads[...], NT, preferred_element_type=F32)

    def cut(t, i):
        return t[i * PART:(i + 1) * PART]

    def rs_copy(f, s, k):
        way = flows[f][0]
        return pltpu.make_async_remote_copy(
            src_ref=rs_out.at[f, s, k], dst_ref=rs_in.at[f, s, k],
            send_sem=rsend.at[f, s, k], recv_sem=rrecv.at[f, s, k],
            device_id=(me, (z + way + 8) % 8), device_id_type=MESH,
        )

    def rs_block(f, s):
        way, hops = flows[f]
        return (z + (hops - s) * way + 8) % 8

    def rs_first(p):
        for f in range(2):
            t = term(rs_block(f, 0), p)
            for i, k in enumerate(parts[p]):
                rs_out[f, 0, k] = cut(t, i).astype(BF16)
                rs_copy(f, 0, k).start()

    def rs_step(s, p):
        live = [f for f in range(2) if s < flows[f][1]]
        terms = {f: term(rs_block(f, s), p) for f in live}
        for i, k in enumerate(parts[p]):
            for f in live:
                rs_copy(f, s - 1, k).wait_recv()
                rs_out[f, s, k] = (rs_in[f, s - 1, k].astype(F32) + cut(terms[f], i)).astype(BF16)
                rs_copy(f, s, k).start()

    def spans(p, i):
        n = 2 * HALVES[p]
        lo, end = i * PART, (i + 1) * PART
        while lo < end:
            hi = min(end, (lo // n + 1) * n)
            to = lo // n * 160 + lo % n + (96 if p else 0)
            yield slice(lo - i * PART, hi - i * PART), slice(to, to + hi - lo)
            lo = hi

    def rs_own(p):
        t = term(z, p)
        for i, k in enumerate(parts[p]):
            rs_copy(1, 2, k).wait_recv()
            total = cut(t, i) + rs_in[1, 2, k].astype(F32)
            for src, dst in spans(p, i):
                outt[dst, :] = total[src]

    def rs_last():
        for p in range(2):
            for i, k in enumerate(parts[p]):
                rs_copy(0, 3, k).wait_recv()
                for src, dst in spans(p, i):
                    outt[dst, :] = outt[dst, :] + rs_in[0, 3, k, src].astype(F32)
        for j in range(NH):
            sl = slice(j * HD, (j + 1) * HD)
            outb[:, sl] = (hid_s[:, sl].astype(F32) + outt[sl, :].T).astype(BF16)

    def masks():
        length = len_ref[me]
        col = lax.broadcasted_iota(jnp.int32, (8, CAP), 1)
        bias[...] = jnp.where(col < length, 0.0, NEG).astype(F32)
        ri = lax.broadcasted_iota(jnp.int32, (ROWS, ROWS), 0)
        ci = lax.broadcasted_iota(jnp.int32, (ROWS, ROWS), 1)
        caus[...] = jnp.where(ci <= ri, 0.0, NEG).astype(F32)

    for cp in wcopies:
        cp.wait()
    pl.semaphore_wait(barrier, len(nbrs))
    stage(0, 0)
    stage(1, 0)
    masks()
    for cp in small[:3]:
        cp.wait()
    head_stage(0)
    head_stage(1)
    stage(0, 1)
    head_stage(2)
    stage(0, 2)
    stage(1, 1)
    stage(0, 3)
    head_stage(3)
    stage(0, 4)
    stage(1, 2)
    head_stage(4)
    stage(0, 5)
    stage(0, 6)
    stage(1, 3)
    head_stage(5)
    stage(0, 7)
    rs_first(0)
    stage(1, 4)
    for cp in own_text:
        cp.wait()
    stage(1, 5)
    stage(2, 0)
    stage(1, 6)
    stage(1, 7)
    rs_first(1)
    for cp in small[3:]:
        cp.wait()
    rs_step(1, 0)
    stage(2, 1)
    rs_step(1, 1)
    stage(2, 2)
    rs_step(2, 0)
    stage(2, 3)
    rs_step(2, 1)
    stage(2, 4)
    stage(2, 5)
    stage(2, 6)
    rs_step(3, 0)
    rs_own(0)
    rs_step(3, 1)
    stage(2, 7)
    rs_own(1)
    for h in range(NH):
        cross_head(h)
    rs_last()
    for ps in pairs:
        for g in ps:
            g.wait_send()
    for p in range(2):
        for k in parts[p]:
            for f in range(2):
                for s in range(flows[f][1]):
                    rs_copy(f, s, k).wait_send()


def per_device(
    hidden, q_new, k_new, v_new, cache_k, cache_v, cache_len, w_out, q_cross, text_k, text_v, prompt_of,
):
    any_spec = pl.BlockSpec(memory_space=pl.ANY)
    smem = pl.BlockSpec(memory_space=pltpu.SMEM)
    v = pltpu.VMEM
    dma = pltpu.SemaphoreType.DMA
    vmem = pl.BlockSpec(memory_space=pltpu.VMEM)
    return pl.pallas_call(
        kernel,
        out_shape=(v((ROWS, W), BF16), v((ROWS, W), BF16)),
        in_specs=[smem, smem] + [any_spec] * 10,
        out_specs=(vmem, vmem),
        scratch_shapes=[
            v((ROWS, W), BF16), v((ROWS, W), BF16), v((ROWS, W), BF16), v((ROWS, W), BF16), v((ROWS, W), BF16),
            v((NH, CAP, HD), BF16), v((NH, CAP, HD), BF16),
            v((64 * HALVES[0], W), BF16), v((64 * HALVES[1], W), BF16),
            v((32, 4, 16, W), BF16), v((32, 4, 16, W), BF16),
            v((2, ROWS, KEYS), F32), v((8, CAP), F32), v((ROWS, ROWS), F32),
            v((ROWS, HD), F32), v((ROWS, HD), F32), v((ROWS, HD), F32), v((ROWS, HD), F32),
            v((ROWS, W), BF16), v((W, ROWS), F32),
            v((2, 4, NH, PART, ROWS), BF16), v((2, 4, NH, PART, ROWS), BF16),
            dma((9,)), dma((2, NH)), dma((3, 2, 16)), dma((3, 2)), dma((3, 2)), dma((2, 4, NH)), dma((2, 4, NH)),
        ],
        compiler_params=pltpu.CompilerParams(
            collective_id=0, has_side_effects=True, vmem_limit_bytes=56 * 1024 * 1024
        ),
    )(cache_len, prompt_of, hidden, q_new, k_new, v_new, cache_k, cache_v, w_out.T, q_cross, text_k, text_v)


def solution(mesh):
    placed = (
        P("req", "tp"), P("req", "tp"), P("req", "tp"), P("req", "tp"),
        P("req", None, "tp"), P("req", None, "tp"),
        P(), P("tp", "req"), P("req", "tp"),
        P(None, "req", "tp"), P(None, "req", "tp"), P("req"),
    )
    return jax.shard_map(
        per_device,
        mesh=mesh,
        in_specs=placed,
        out_specs=(P("req", "tp"), P("req", "tp")),
        check_vma=False,
    )
```

```python
import jax
import jax.numpy as jnp
from jax import lax
from jax.experimental import pallas as pl
from jax.experimental.pallas import tpu as pltpu
from jax.sharding import PartitionSpec as P

MESH = pl.DeviceIdType.MESH
HD = 128
NH = 5
ROWS = 256
W = NH * HD
CAP = 4096
KEYS = CAP + ROWS
CHUNK = 1024
TILES = CHUNK // HD
TURN = 160
NEG = -1e30
SCALE = HD**-0.5
LOG2E = 1.4426950408889634
NT = (((1,), (1,)), ((), ()))
F32 = jnp.float32
BF16 = jnp.bfloat16


def kernel(
    len_ref, prompt_ref, hid_h, q_h, kn_h, vn_h, ck_h, cv_h, w_h, qc_h, tk_h, tv_h,
    outb, crossb,
    q_s, kn_s, vn_s, hid_s, qc_s, k_s, v_s, wall, tk, tv, sbuf, bias, caus,
    mrun, mfin, lrun, acc, heads, outt, rs_in, rs_out,
    lsem, kvsem, grecv, gsib, gsend, rrecv, rsend,
):
    me = lax.axis_index("req")
    z = lax.axis_index("tp")
    x, y, c = me // 8, (me // 2) % 4, me % 2
    d = 1 - 2 * c

    def rid(ax, ay, ac):
        return (((ax + 8) % 4) * 4 + (ay + 8) % 4) * 2 + ac

    sib = (rid(x, y, 1 - c), z)
    zp = (me, (z + 1) % 8)
    zm = (me, (z + 7) % 8)

    def shift(axis, by):
        if axis == "x":
            return (rid(x + by, y, c), z)
        return (rid(x, y + by, c), z)

    mine = pl.multiple_of(me * 160, 32)
    wcopy = pltpu.make_async_copy(w_h, wall.at[pl.ds(mine, 160)], lsem.at[0])
    wcopy.start()
    small = [
        pltpu.make_async_copy(src, dst, lsem.at[i])
        for i, (src, dst) in enumerate([(q_h, q_s), (kn_h, kn_s), (vn_h, vn_s), (hid_h, hid_s), (qc_h, qc_s)], 1)
    ]
    for cp in small[:3]:
        cp.start()

    def kv_copy(h):
        return (
            pltpu.make_async_copy(ck_h.at[0, :, pl.ds(h * HD, HD)], k_s.at[h], kvsem.at[0, h]),
            pltpu.make_async_copy(cv_h.at[0, :, pl.ds(h * HD, HD)], v_s.at[h], kvsem.at[1, h]),
        )

    kv = [kv_copy(h) for h in range(NH)]
    for kc, vc in kv:
        kc.start()
        vc.start()
    own_text = (
        pltpu.make_async_copy(tk_h, tk.at[me], lsem.at[6]),
        pltpu.make_async_copy(tv_h, tv.at[me], lsem.at[7]),
    )
    for cp in own_text:
        cp.start()
    for cp in small[3:]:
        cp.start()

    barrier = pltpu.get_barrier_semaphore()
    nbrs = (shift("x", 1), shift("x", -1), shift("y", 1), shift("y", -1), sib, zp, zm)
    for nb in nbrs:
        pl.semaphore_signal(barrier, inc=1, device_id=nb, device_id_type=MESH)

    def piece(p, ab, ax, ay, ac):
        r = rid(ax, ay, ac)
        if p == 0:
            return wall.at[pl.ds(pl.multiple_of(r * 160 + ab * 80, 16), 80)]
        return (tk if ab == 0 else tv).at[r]

    def some(p, ab, n):
        if p == 0:
            return wall.at[pl.ds(0, 80 * n)]
        return (tk if ab == 0 else tv).at[pl.ds(0, n)]

    class Gather:
        def __init__(self, p, ab):
            self.p, self.ab = p, ab
            self.f, self.g = ("y", "x") if ab == 0 else ("x", "y")

        def ref(self, rf, rg):
            if self.ab == 0:
                return piece(self.p, self.ab, x + rg, y + rf, c)
            return piece(self.p, self.ab, x + rf, y + rg, c)

        def copy(self, ref, dev, rf, rg):
            return pltpu.make_async_remote_copy(
                src_ref=ref, dst_ref=ref,
                send_sem=gsend.at[self.p, self.ab],
                recv_sem=grecv.at[self.p, self.ab, (rf % 4) * 4 + rg % 4],
                device_id=dev, device_id_type=MESH,
            )

        def to_f(self, rf, rg, by, nf):
            self.copy(self.ref(rf, rg), shift(self.f, by), nf, 0).start()

        def to_g(self, rf, rg, by, nf, ng):
            self.copy(self.ref(rf, rg), shift(self.g, by), nf, ng).start()

        def both_g(self, rf):
            for by in (1, -1):
                self.to_g(rf, 0, by, rf, -by)

        def to_sib(self, rf, rg):
            ref = self.ref(rf, rg)
            pltpu.make_async_remote_copy(
                src_ref=ref, dst_ref=ref,
                send_sem=gsend.at[self.p, self.ab],
                recv_sem=gsib.at[self.p, self.ab],
                device_id=sib, device_id_type=MESH,
            ).start()

        def wait(self, rf, rg):
            self.copy(self.ref(rf, rg), sib, rf, rg).wait_recv()

        def wait_sib(self):
            ref = some(self.p, self.ab, 16)
            pltpu.make_async_remote_copy(
                src_ref=ref, dst_ref=ref,
                send_sem=gsend.at[self.p, self.ab],
                recv_sem=gsib.at[self.p, self.ab],
                device_id=sib, device_id_type=MESH,
            ).wait_recv()

        def wait_send(self):
            self.copy(some(self.p, self.ab, 31), sib, 0, 0).wait_send()

    pairs = [(Gather(0, 0), Gather(0, 1)), (Gather(1, 0), Gather(1, 1))]

    def stage(p, n):
        gs = pairs[p]
        if n == 0:
            for g in gs:
                for by in (1, -1):
                    g.to_f(0, 0, by, -by)
            for g in gs:
                g.both_g(0)
            for g in gs:
                g.to_sib(0, 0)
        elif n == 1:
            for g in gs:
                g.wait(1, 0)
                g.wait(3, 0)
                g.to_f(-d, 0, d, 2)
            for g in gs:
                g.both_g(1)
                g.both_g(3)
            for g in gs:
                g.to_sib(1, 0)
                g.to_sib(3, 0)
        elif n == 2:
            for g in gs:
                g.wait(2, 0)
                g.both_g(2)
            for g in gs:
                g.to_sib(2, 0)
        elif n == 3:
            for g in gs:
                for rf in (1, 3):
                    g.wait(rf, 1)
                    g.wait(rf, 3)
                    g.to_g(rf, -d, d, rf, 2)
            for g in gs:
                for rf in (1, 3):
                    g.to_sib(rf, 1)
                    g.to_sib(rf, 3)
        elif n == 4:
            for g in gs:
                g.wait(2, 1)
                g.wait(2, 3)
                g.to_g(2, -d, d, 2, 2)
            for g in gs:
                g.wait(0, 1)
                g.wait(0, 3)
                g.to_g(0, -d, d, 0, 2)
            for g in gs:
                for rg in (1, 3):
                    g.to_sib(2, rg)
                    g.to_sib(0, rg)
        elif n == 5:
            for g in gs:
                for rf in (1, 3):
                    g.wait(rf, 2)
                    g.to_sib(rf, 2)
        elif n == 6:
            for g in gs:
                g.wait(2, 2)
                g.wait(0, 2)
            for g in gs:
                g.to_sib(2, 2)
                g.to_sib(0, 2)
        else:
            for g in gs:
                g.wait_sib()

    def qk_new(h):
        sl = slice(h * HD, (h + 1) * HD)
        s = lax.dot_general(q_s[:, sl], kn_s[:, sl], NT, preferred_element_type=F32)
        s = s + caus[...]
        sbuf[h % 2, :, CAP:KEYS] = s
        mrun[...] = jnp.maximum(s[:, 0:128], s[:, 128:256])

    def qk_chunk(h, i):
        sl = slice(h * HD, (h + 1) * HD)
        at = pl.multiple_of(i * CHUNK, CHUNK)
        s = lax.dot_general(q_s[:, sl], k_s[h, pl.ds(at, CHUNK), :], NT, preferred_element_type=F32)
        s = s + bias[0:1, pl.ds(at, CHUNK)]
        sbuf[h % 2, :, pl.ds(at, CHUNK)] = s
        m = mrun[...]
        for t in range(TILES):
            m = jnp.maximum(m, s[:, t * HD:(t + 1) * HD])
        mrun[...] = m

    def set_max():
        mfin[...] = jnp.broadcast_to(jnp.max(mrun[...], axis=1, keepdims=True), (ROWS, HD))

    def pv(p, v, lane_tiles):
        part = p[:, 0:128]
        for t in range(1, lane_tiles):
            part = part + p[:, t * 128:(t + 1) * 128]
        return part, jnp.dot(p.astype(BF16), v, preferred_element_type=F32)

    def weigh(s, lane_tiles):
        m = mfin[...]
        return jnp.concatenate(
            [jnp.exp2((s[:, t * 128:(t + 1) * 128] - m) * (SCALE * LOG2E)) for t in range(lane_tiles)], axis=1
        )

    def pv_new(h):
        sl = slice(h * HD, (h + 1) * HD)
        p = weigh(sbuf[h % 2, :, CAP:KEYS], 2)
        part, o = pv(p, vn_s[:, sl], 2)
        lrun[...] = part
        acc[...] = o

    def pv_chunk(h, i):
        at = pl.multiple_of(i * CHUNK, CHUNK)
        p = weigh(sbuf[h % 2, :, pl.ds(at, CHUNK)], TILES)
        part, o = pv(p, v_s[h, pl.ds(at, CHUNK), :], TILES)
        lrun[...] += part
        acc[...] += o

    def head_stage(h):
        if h < NH:
            kv[h][0].wait()
        if h > 0:
            kv[h - 1][1].wait()
            pv_new(h - 1)
        if h < NH:
            qk_new(h)

        @pl.loop(0, CAP // CHUNK)
        def _(i):
            if h < NH:
                qk_chunk(h, i)
            if h > 0:
                pv_chunk(h - 1, i)

        if h > 0:
            mass = jnp.sum(lrun[...], axis=1, keepdims=True)
            heads[:, (h - 1) * HD:h * HD] = (acc[...] / mass).astype(BF16)
        if h < NH:
            set_max()

    prompt = prompt_ref[0]

    def cross_head(h):
        sl = slice(h * HD, (h + 1) * HD)
        kt = tk[:, prompt, :, sl].reshape(512, HD)
        vt = tv[:, prompt, :, sl].reshape(512, HD)
        s = lax.dot_general(qc_s[:, sl], kt, NT, preferred_element_type=F32)
        m = jnp.max(s, axis=1, keepdims=True)
        p = jnp.exp2((s - m) * (SCALE * LOG2E))
        mass = jnp.sum(p, axis=1, keepdims=True)
        o = jnp.dot(p.astype(BF16), vt, preferred_element_type=F32)
        crossb[:, sl] = (o / mass).astype(BF16)

    flows = ((d, 4), (-d, 3))
    PARTS = W // TURN

    def term(b, k):
        at = pl.multiple_of(b * W + k * TURN, 32)
        return lax.dot_general(wall[pl.ds(at, TURN), :], heads[...], NT, preferred_element_type=F32)

    def rs_copy(f, s, k):
        way = flows[f][0]
        return pltpu.make_async_remote_copy(
            src_ref=rs_out.at[f, s, k], dst_ref=rs_in.at[f, s, k],
            send_sem=rsend.at[f, s, k], recv_sem=rrecv.at[f, s, k],
            device_id=(me, (z + way + 8) % 8), device_id_type=MESH,
        )

    def rs_block(f, s):
        way, hops = flows[f]
        return (z + (hops - s) * way + 8) % 8

    def rs_first():
        for k in range(PARTS):
            for f in range(2):
                rs_out[f, 0, k] = term(rs_block(f, 0), k).astype(BF16)
                rs_copy(f, 0, k).start()

    def rs_step(s):
        for k in range(PARTS):
            for f in range(2):
                if s < flows[f][1]:
                    t = term(rs_block(f, s), k)
                    rs_copy(f, s - 1, k).wait_recv()
                    rs_out[f, s, k] = (rs_in[f, s - 1, k].astype(F32) + t).astype(BF16)
                    rs_copy(f, s, k).start()

    def rs_own():
        for k in range(PARTS):
            t = term(z, k)
            rs_copy(1, 2, k).wait_recv()
            outt[k * TURN:(k + 1) * TURN, :] = t + rs_in[1, 2, k].astype(F32)

    def rs_last():
        done = 0
        for k in range(PARTS):
            rs_copy(0, 3, k).wait_recv()
            at = slice(k * TURN, (k + 1) * TURN)
            outt[at, :] = outt[at, :] + rs_in[0, 3, k].astype(F32)
            ready = (k + 1) * TURN // HD
            for j in range(done, ready):
                sl = slice(j * HD, (j + 1) * HD)
                outb[:, sl] = (hid_s[:, sl].astype(F32) + outt[sl, :].T).astype(BF16)
            done = ready

    def masks():
        length = len_ref[me]
        col = lax.broadcasted_iota(jnp.int32, (8, CAP), 1)
        bias[...] = jnp.where(col < length, 0.0, NEG).astype(F32)
        ri = lax.broadcasted_iota(jnp.int32, (ROWS, ROWS), 0)
        ci = lax.broadcasted_iota(jnp.int32, (ROWS, ROWS), 1)
        caus[...] = jnp.where(ci <= ri, 0.0, NEG).astype(F32)

    wcopy.wait()
    pl.semaphore_wait(barrier, len(nbrs))
    stage(0, 0)
    masks()
    for cp in small[:3]:
        cp.wait()
    head_stage(0)
    head_stage(1)
    stage(0, 1)
    head_stage(2)
    head_stage(3)
    stage(0, 2)
    head_stage(4)
    stage(0, 3)
    head_stage(5)
    stage(0, 4)
    for cp in own_text:
        cp.wait()
    stage(1, 0)
    stage(0, 5)
    stage(0, 6)
    stage(0, 7)
    rs_first()
    for cp in small[3:]:
        cp.wait()
    stage(1, 1)
    rs_step(1)
    stage(1, 2)
    stage(1, 3)
    rs_step(2)
    stage(1, 4)
    stage(1, 5)
    stage(1, 6)
    rs_step(3)
    stage(1, 7)
    rs_own()
    for h in range(NH):
        cross_head(h)
    rs_last()
    for ps in pairs:
        for g in ps:
            g.wait_send()
    for k in range(PARTS):
        for f in range(2):
            for s in range(flows[f][1]):
                rs_copy(f, s, k).wait_send()


def per_device(
    hidden, q_new, k_new, v_new, cache_k, cache_v, cache_len, w_out, q_cross, text_k, text_v, prompt_of,
):
    any_spec = pl.BlockSpec(memory_space=pl.ANY)
    smem = pl.BlockSpec(memory_space=pltpu.SMEM)
    v = pltpu.VMEM
    dma = pltpu.SemaphoreType.DMA
    vmem = pl.BlockSpec(memory_space=pltpu.VMEM)
    return pl.pallas_call(
        kernel,
        out_shape=(v((ROWS, W), BF16), v((ROWS, W), BF16)),
        in_specs=[smem, smem] + [any_spec] * 10,
        out_specs=(vmem, vmem),
        scratch_shapes=[
            v((ROWS, W), BF16), v((ROWS, W), BF16), v((ROWS, W), BF16), v((ROWS, W), BF16), v((ROWS, W), BF16),
            v((NH, CAP, HD), BF16), v((NH, CAP, HD), BF16),
            v((8 * W, W), BF16),
            v((32, 4, 16, W), BF16), v((32, 4, 16, W), BF16),
            v((2, ROWS, KEYS), F32), v((8, CAP), F32), v((ROWS, ROWS), F32),
            v((ROWS, HD), F32), v((ROWS, HD), F32), v((ROWS, HD), F32), v((ROWS, HD), F32),
            v((ROWS, W), BF16), v((W, ROWS), F32),
            v((2, 4, 4, TURN, ROWS), BF16), v((2, 4, 4, TURN, ROWS), BF16),
            dma((8,)), dma((2, NH)), dma((2, 2, 16)), dma((2, 2)), dma((2, 2)), dma((2, 4, 4)), dma((2, 4, 4)),
        ],
        compiler_params=pltpu.CompilerParams(
            collective_id=0, has_side_effects=True, vmem_limit_bytes=56 * 1024 * 1024
        ),
    )(cache_len, prompt_of, hidden, q_new, k_new, v_new, cache_k, cache_v, w_out.T, q_cross, text_k, text_v)


def solution(mesh):
    placed = (
        P("req", "tp"), P("req", "tp"), P("req", "tp"), P("req", "tp"),
        P("req", None, "tp"), P("req", None, "tp"),
        P(), P("tp", "req"), P("req", "tp"),
        P(None, "req", "tp"), P(None, "req", "tp"), P("req"),
    )
    return jax.shard_map(
        per_device,
        mesh=mesh,
        in_specs=placed,
        out_specs=(P("req", "tp"), P("req", "tp")),
        check_vma=False,
    )
```
